32 devices in a mesh: grp: 2 (over y), lvl: 4 (over x, core), col: 4 (over z).
Axes of the slice: x: 2, y: 2, z: 4, core: 2. Of those that a mesh axis runs over, the one named last changes fastest.
Arguments:
- inverse_diag: float32 [64, 256, 256], P(('grp', 'lvl')), parts along dimension 0, may hold values from 0 to 2, as said below
- down_block: float32 [64, 256, 256], P(('grp', 'lvl')), parts along dimension 0, may hold values from 0 to 2, as said below
- up_block: float32 [64, 256, 256], P(('grp', 'lvl')), parts along dimension 0, may hold values from 0 to 1, as said below
- reward: float32 [64, 64, 256], P(('grp', 'lvl'), 'col'), parts along dimension 0, may hold values from -6 to 6
Outputs:
- values: float32 [64, 64, 256], P(('grp', 'lvl'), 'col'), parts along dimension 0
The draws below stay inside these ranges and needn't reach their ends.
There are 2 independent parts, one for each index of `grp`. The reference program is written for one: setup_inputs(seed, part) draws one part's arguments, and reference() takes and returns one part's arrays. A program takes and returns all parts, laid end to end along the dimension named above; each array names one. Nothing has to cross between parts.
Inputs may be any that keep to these rules, and one draw needn't show every extreme that they name: `inverse_diag`: Nonnegative. `down_block`: Nonnegative. `up_block`: Nonnegative.
All inputs are finite; a program needn't handle non-finite values.
Results may differ from the reference program's by a relative error of at most 0.00011.
Values sent between devices are 32-bit elements; how exact they have to be, the bound alone decides.
A program may use at most 64 MiB of HBM per device.

```python
import math
import jax
import jax.numpy as jnp
import numpy as np
from jax import lax

M = 256
K = 64
SWEEPS = 8
LEVELS = 32


mix_local = 0.2


mix_tail = 0.02


up_strength = 3.0


def level_scale(key):
    spread = jax.random.uniform(jax.random.fold_in(key, 17), (LEVELS, 1, 1), jnp.float32, math.log(0.5), math.log(2.0))
    return jnp.exp(spread)


def keep_rate():
    keep_share = 0.3
    return keep_share ** (1.0 / LEVELS)


def local_table():
    offsets = np.abs(np.arange(M)[:, None] - np.arange(M)[None, :])
    weights = np.where((offsets > 0) & (offsets <= 4), 5.0 - offsets, 0.0)
    weights = weights / weights.sum(axis=1, keepdims=True)
    return jnp.asarray(weights, dtype=jnp.float32)


def phase_mixing(key):
    local_low, local_high, tail_low, tail_high = (0.5, 1.5, 0.0, 2.0)
    local_noise = jax.random.uniform(jax.random.fold_in(key, 1), (LEVELS, M, M), jnp.float32, local_low, local_high)
    tail_noise = jax.random.uniform(jax.random.fold_in(key, 2), (LEVELS, M, M), jnp.float32, tail_low, tail_high)
    diag_noise = jax.random.uniform(jax.random.fold_in(key, 3), (LEVELS, M), jnp.float32, 0.9, 1.1)
    identity_mat = jnp.eye(M, dtype=jnp.float32)
    own_part = (1.0 - mix_local - mix_tail) * diag_noise[:, :, None] * identity_mat[None, :, :]
    near_part = mix_local * local_noise * local_table()[None, :, :]
    far_part = mix_tail / M * tail_noise
    return own_part + near_part + far_part


def draw_inverse_diag(key, part):
    return phase_mixing(jax.random.fold_in(key, 101)) * (keep_rate() / level_scale(key))


def draw_down_block(key, part):
    return phase_mixing(jax.random.fold_in(key, 202)) * level_scale(key)


def draw_up_block(key, part):
    return phase_mixing(jax.random.fold_in(key, 303)) * level_scale(key) * (up_strength / max(LEVELS, 32))


def level_of(rng, dims, pieces, smallest, top_value):
    gain = 1.0
    for position, parts in pieces:
        draws = jax.random.uniform(jax.random.fold_in(jax.random.fold_in(rng, 6), position), (parts,), jnp.float32, smallest / len(pieces), top_value / len(pieces))
        gain = gain * jnp.repeat(jnp.exp(draws), dims[position] // parts).reshape((-1,) + (1,) * (len(dims) - 1 - position))
    return gain


def gaussian(own_key, shape, scale, most, split=(), held_as=jnp.bfloat16):
    result = jax.random.normal(own_key, shape, jnp.float32) * scale
    if len(split) > 0:
        result = level_of(own_key, shape, split, -0.22, 0.18) * result
    return jnp.clip(result, min=-most, max=most).astype(held_as)


def setup_inputs(seed: int = 0, part: int = 0) -> dict:
    key_list = jax.random.split(jax.random.key(seed), 5)
    part_keys = jax.random.split(jax.random.fold_in(key_list[4], part), 5)
    return {
        "inverse_diag": draw_inverse_diag(jax.random.fold_in(jax.random.fold_in(key_list[4], part), 71), part),
        "down_block": draw_down_block(jax.random.fold_in(jax.random.fold_in(key_list[4], part), 71), part),
        "up_block": draw_up_block(jax.random.fold_in(jax.random.fold_in(key_list[4], part), 71), part),
        "reward": gaussian(part_keys[3], (LEVELS, K, M), 1.0, 6.0, ((0, 4), (1, 4)), jnp.float32),
    }


PRECISE = lax.Precision.HIGHEST


def apply_right(vector, matrix):
    return jnp.einsum("km,pm->kp", vector, matrix, precision=PRECISE)


def one_sweep(estimate, inverse_diag, down_block, up_block, reward):
    shifted = jnp.concatenate([estimate[1:], jnp.zeros_like(estimate[:1])], axis=0)

    def level_step(carried, inputs):
        inv_here, down_here, up_here, pay_here, next_old = inputs
        updated = apply_right(pay_here + apply_right(carried, down_here) + apply_right(next_old, up_here), inv_here)
        return updated, updated

    _, stacked = lax.scan(level_step, jnp.zeros_like(estimate[0]), (inverse_diag, down_block, up_block, reward, shifted))
    return stacked


def reference(inverse_diag, down_block, up_block, reward):
    estimate = jnp.zeros_like(reward)
    for repeat in range(SWEEPS):
        estimate = one_sweep(estimate, inverse_diag, down_block, up_block, reward)
    return estimate
```

```python
import functools

import jax
import jax.numpy as jnp
from jax import lax
from jax.experimental import pallas as pl
from jax.experimental.pallas import tpu as pltpu
from jax.sharding import PartitionSpec as P

SWEEPS = 8
MESH = pl.DeviceIdType.MESH


def split(value):
    high = value.astype(jnp.bfloat16)
    low = (value - high.astype(jnp.float32)).astype(jnp.bfloat16)
    return high, low


def dot(left, right):
    return jnp.dot(left, right, preferred_element_type=jnp.float32)


def apply_split(vector, high, low):
    rows = vector.shape[0]
    rounded = vector.astype(jnp.bfloat16).astype(jnp.float32)
    stacked = jnp.concatenate([rounded, vector - rounded], axis=0).astype(jnp.bfloat16)
    both = dot(stacked, high)
    return both[:rows] + both[rows:] + dot(rounded.astype(jnp.bfloat16), low)


def kernel(
    count, inv_hbm, down_hbm, up_hbm, reward_ref, out_ref,
    inv, down, up, a_high, a_low, b_high, b_low, base, from_below, from_above, top, bottom,
    load_sem, below_recv, above_recv, top_send, bottom_send,
):
    levels, phases = inv_hbm.shape[0], inv_hbm.shape[1]
    place = lax.axis_index("lvl")
    first, last = place == 0, place == count - 1

    def loads(level):
        return [
            pltpu.make_async_copy(source.at[level], target.at[level], load_sem.at[kind, level])
            for kind, (source, target) in enumerate(
                ((inv_hbm, inv), (down_hbm, down), (up_hbm, up))
            )
        ]

    for level in range(levels):
        for copy in loads(level):
            copy.start()

    barrier = pltpu.get_barrier_semaphore()

    @pl.when(place > 0)
    def _():
        pl.semaphore_signal(barrier, inc=1, device_id={"lvl": place - 1}, device_id_type=MESH)

    @pl.when(place < count - 1)
    def _():
        pl.semaphore_signal(barrier, inc=1, device_id={"lvl": place + 1}, device_id_type=MESH)

    out_ref[...] = jnp.zeros_like(out_ref)

    @pl.when(first)
    def _():
        from_below[...] = jnp.zeros_like(from_below)

    @pl.when(last)
    def _():
        from_above[...] = jnp.zeros_like(from_above)

    @pl.when(place < count - 1)
    def _():
        from_above[0] = jnp.zeros_like(from_above[0])

    for level in range(levels):
        for copy in loads(level):
            copy.wait()
        inv_t_high, inv_t_low = split(inv[level].T)
        base[level] = apply_split(reward_ref[level], inv_t_high, inv_t_low)
        for block, high_ref, low_ref in ((down, a_high, a_low), (up, b_high, b_low)):
            block_high, block_low = split(block[level].T)
            product = dot(block_high, inv_t_high) + (
                dot(block_high, inv_t_low) + dot(block_low, inv_t_high)
            )
            high_ref[level], low_ref[level] = split(product)

    pl.semaphore_wait(barrier, jnp.minimum(place, 1) + jnp.minimum(count - 1 - place, 1))

    def going_up(sweep):
        return pltpu.make_async_remote_copy(
            src_ref=top.at[sweep], dst_ref=from_below.at[sweep],
            send_sem=top_send.at[sweep], recv_sem=below_recv.at[sweep],
            device_id={"lvl": place + 1}, device_id_type=MESH,
        )

    def going_down(sweep):
        return pltpu.make_async_remote_copy(
            src_ref=bottom.at[sweep], dst_ref=from_above.at[sweep + 1],
            send_sem=bottom_send.at[sweep], recv_sem=above_recv.at[sweep],
            device_id={"lvl": place - 1}, device_id_type=MESH,
        )

    def one_sweep(sweep, _):
        terms = [
            base[level] + apply_split(out_ref[level + 1], b_high[level], b_low[level])
            for level in range(levels - 1)
        ]

        @pl.when(place > 0)
        def _():
            going_up(sweep).wait_recv()

        carried = terms[0] + apply_split(from_below[sweep], a_high[0], a_low[0])
        out_ref[0] = carried

        @pl.when((place > 0) & (sweep < SWEEPS - 1))
        def _():
            bottom[sweep] = carried
            going_down(sweep).start()

        for level in range(1, levels - 1):
            carried = terms[level] + apply_split(carried, a_high[level], a_low[level])
            out_ref[level] = carried
        end = levels - 1
        partial = base[end] + apply_split(carried, a_high[end], a_low[end])

        @pl.when((place < count - 1) & (sweep > 0))
        def _():
            going_down(sweep - 1).wait_recv()

        carried = partial + apply_split(from_above[sweep], b_high[end], b_low[end])
        out_ref[end] = carried

        @pl.when(place < count - 1)
        def _():
            top[sweep] = carried
            going_up(sweep).start()

        return 0

    lax.fori_loop(0, SWEEPS, one_sweep, 0)

    for sweep in range(SWEEPS):
        @pl.when(place < count - 1)
        def _():
            going_up(sweep).wait_send()

        if sweep < SWEEPS - 1:
            @pl.when(place > 0)
            def _():
                going_down(sweep).wait_send()


def solution(mesh):
    count = mesh.shape["lvl"]

    def local(inverse_diag, down_block, up_block, reward):
        levels, rows, phases = reward.shape
        whole = (levels, phases, phases)
        wide = pltpu.VMEM(whole, jnp.float32)
        narrow = pltpu.VMEM(whole, jnp.bfloat16)
        edge = pltpu.VMEM((SWEEPS, rows, phases), jnp.float32)
        return pl.pallas_call(
            functools.partial(kernel, count),
            out_shape=jax.ShapeDtypeStruct(reward.shape, jnp.float32),
            in_specs=[pl.BlockSpec(memory_space=pl.ANY)] * 3
            + [pl.BlockSpec(memory_space=pltpu.VMEM)],
            out_specs=pl.BlockSpec(memory_space=pltpu.VMEM),
            scratch_shapes=[wide] * 3 + [narrow] * 4
            + [pltpu.VMEM(reward.shape, jnp.float32)] + [edge] * 4
            + [pltpu.SemaphoreType.DMA((3, levels))] + [pltpu.SemaphoreType.DMA((SWEEPS,))] * 4,
            compiler_params=pltpu.CompilerParams(
                collective_id=0, has_side_effects=True, vmem_limit_bytes=40 << 20
            ),
            name="sweeps",
        )(inverse_diag, down_block, up_block, reward)

    matrices = P(("grp", "lvl"), None, None)
    columns = P(("grp", "lvl"), "col", None)
    return jax.shard_map(
        local, mesh=mesh, in_specs=(matrices, matrices, matrices, columns),
        out_specs=columns, check_vma=False,
    )
```

```python
import functools

import jax
import jax.numpy as jnp
from jax import lax
from jax.experimental import pallas as pl
from jax.experimental.pallas import tpu as pltpu
from jax.sharding import PartitionSpec as P

SWEEPS = 8
MESH = pl.DeviceIdType.MESH


def split(value):
    high = value.astype(jnp.bfloat16)
    low = (value - high.astype(jnp.float32)).astype(jnp.bfloat16)
    return high, low


def dot(left, right):
    return jnp.dot(left, right, preferred_element_type=jnp.float32)


def apply_split(vector, high, low):
    rows = vector.shape[0]
    rounded = vector.astype(jnp.bfloat16).astype(jnp.float32)
    stacked = jnp.concatenate([rounded, vector - rounded], axis=0).astype(jnp.bfloat16)
    both = dot(stacked, high)
    return both[:rows] + both[rows:] + dot(rounded.astype(jnp.bfloat16), low)


def kernel(
    count, inv_hbm, down_hbm, up_hbm, reward_ref, out_ref,
    inv, down, up, a_high, a_low, b_high, b_low, base, from_below, from_above, top, bottom,
    edge_out, edge_in,
    load_sem, below_recv, above_recv, top_send, bottom_send, edge_send, edge_recv,
):
    levels = inv_hbm.shape[0]
    place = lax.axis_index("lvl")
    has_below, has_above = place > 0, place < count - 1
    at = dict(device_id_type=MESH)
    end = levels - 1

    def loads(level):
        return [
            pltpu.make_async_copy(source.at[level], target.at[level], load_sem.at[kind, level])
            for kind, (source, target) in enumerate(
                ((inv_hbm, inv), (down_hbm, down), (up_hbm, up))
            )
        ]

    for level in range(levels):
        for copy in loads(level):
            copy.start()

    barrier = pltpu.get_barrier_semaphore()

    @pl.when(has_below)
    def _():
        pl.semaphore_signal(barrier, inc=1, device_id={"lvl": place - 1}, **at)

    @pl.when(has_above)
    def _():
        pl.semaphore_signal(barrier, inc=1, device_id={"lvl": place + 1}, **at)

    out_ref[...] = jnp.zeros_like(out_ref)
    from_above[0:2] = jnp.zeros_like(from_above[0:2])

    @pl.when(place == 0)
    def _():
        from_below[...] = jnp.zeros_like(from_below)

    @pl.when(place == count - 1)
    def _():
        from_above[...] = jnp.zeros_like(from_above)
        edge_in[...] = jnp.zeros_like(edge_in)
        base[levels] = jnp.zeros_like(base[levels])

    def edge_copies():
        below = {"lvl": place - 1}
        pairs = (
            (base.at[0], base.at[levels]),
            (edge_out.at[0], edge_in.at[0]),
            (edge_out.at[1], edge_in.at[1]),
        )
        return [
            pltpu.make_async_remote_copy(
                src_ref=source, dst_ref=target, send_sem=edge_send.at[n], recv_sem=edge_recv.at[n],
                device_id=below, **at,
            )
            for n, (source, target) in enumerate(pairs)
        ]

    for level in range(levels):
        for copy in loads(level):
            copy.wait()
        inv_t_high, inv_t_low = split(inv[level].T)
        base[level] = apply_split(reward_ref[level], inv_t_high, inv_t_low)
        for kind, (block, high_ref, low_ref) in enumerate(
            ((down, a_high, a_low), (up, b_high, b_low))
        ):
            block_high, block_low = split(block[level].T)
            product = dot(block_high, inv_t_high) + (
                dot(block_high, inv_t_low) + dot(block_low, inv_t_high)
            )
            high_ref[level], low_ref[level] = split(product)
            if level == 0:
                edge_out[kind] = product
        if level == 0:
            pl.semaphore_wait(
                barrier, jnp.minimum(place, 1) + jnp.minimum(count - 1 - place, 1)
            )

            @pl.when(has_below)
            def _():
                for copy in edge_copies():
                    copy.start()

    def going_up(sweep):
        return pltpu.make_async_remote_copy(
            src_ref=top.at[sweep], dst_ref=from_below.at[sweep],
            send_sem=top_send.at[sweep], recv_sem=below_recv.at[sweep],
            device_id={"lvl": place + 1}, **at,
        )

    def going_down(sweep):
        return pltpu.make_async_remote_copy(
            src_ref=bottom.at[sweep], dst_ref=from_above.at[sweep + 2],
            send_sem=bottom_send.at[sweep], recv_sem=above_recv.at[sweep],
            device_id={"lvl": place - 1}, **at,
        )

    def await_below(sweep):
        @pl.when(has_below)
        def _():
            going_up(sweep).wait_recv()

        return from_below[sweep]

    def await_above(turn, sweep):
        @pl.when(has_above & (turn > 0))
        def _():
            going_down(sweep - 2).wait_recv()

        return from_above[sweep]

    def send_up(sweep, value):
        @pl.when(has_above)
        def _():
            top[sweep] = value
            going_up(sweep).start()

    def send_down(turn, sweep, value):
        @pl.when(has_below & (turn < SWEEPS // 2 - 1))
        def _():
            bottom[sweep] = value
            going_down(sweep).start()

    def times_a(value, level):
        return apply_split(value, a_high[level], a_low[level])

    def times_b(value, level):
        return apply_split(value, b_high[level], b_low[level])

    def two_sweeps(turn, _):
        even, odd = 2 * turn, 2 * turn + 1
        terms = [base[n] + times_b(out_ref[n + 1], n) for n in range(end)]
        old_end = out_ref[end]
        x, y = [None] * (levels + 1), [None] * levels

        x[0] = terms[0] + times_a(await_below(even), 0)
        x[1] = terms[1] + times_a(x[0], 1)
        send_down(turn, even, x[1])
        entering = await_below(odd)
        for step in range(2, end):
            low = step - 2
            x[step] = terms[step] + times_a(x[step - 1], step)
            y[low] = (base[low] + times_b(x[low + 1], low)) + times_a(
                entering if low == 0 else y[low - 1], low
            )
            if low == 1:
                send_down(turn, odd, y[1])

        @pl.when(turn == 0)
        def _():
            @pl.when(has_above)
            def _():
                for copy in edge_copies():
                    copy.wait_recv()

            a_high[levels], a_low[levels] = split(edge_in[0])
            b_high[levels], b_low[levels] = split(edge_in[1])

        after = base[levels] + times_a(old_end, levels) + times_b(await_above(turn, even), levels)
        after = jnp.where(turn > 0, after, jnp.zeros_like(after))
        x[end] = (base[end] + times_a(x[end - 1], end)) + times_b(after, end)
        send_up(even, x[end])
        low = end - 2
        y[low] = (base[low] + times_b(x[low + 1], low)) + times_a(y[low - 1], low)
        beyond = base[levels] + times_b(await_above(turn, odd), levels)
        x[levels] = beyond + times_a(x[end], levels)
        low = end - 1
        y[low] = (base[low] + times_b(x[end], low)) + times_a(y[low - 1], low)
        y[end] = (base[end] + times_a(y[end - 1], end)) + times_b(x[levels], end)
        send_up(odd, y[end])
        for n in range(levels):
            out_ref[n] = y[n]
        return 0

    lax.fori_loop(0, SWEEPS // 2, two_sweeps, 0)

    @pl.when(has_above)
    def _():
        for sweep in range(SWEEPS):
            going_up(sweep).wait_send()

    @pl.when(has_below)
    def _():
        for sweep in range(SWEEPS - 2):
            going_down(sweep).wait_send()
        for copy in edge_copies():
            copy.wait_send()


def solution(mesh):
    count = mesh.shape["lvl"]

    def local(inverse_diag, down_block, up_block, reward):
        levels, rows, phases = reward.shape
        whole = (levels, phases, phases)
        wide = pltpu.VMEM(whole, jnp.float32)
        narrow = pltpu.VMEM((levels + 1, phases, phases), jnp.bfloat16)
        edge = pltpu.VMEM((SWEEPS, rows, phases), jnp.float32)
        return pl.pallas_call(
            functools.partial(kernel, count),
            out_shape=jax.ShapeDtypeStruct(reward.shape, jnp.float32),
            in_specs=[pl.BlockSpec(memory_space=pl.ANY)] * 3
            + [pl.BlockSpec(memory_space=pltpu.VMEM)],
            out_specs=pl.BlockSpec(memory_space=pltpu.VMEM),
            scratch_shapes=[wide] * 3 + [narrow] * 4
            + [pltpu.VMEM((levels + 1, rows, phases), jnp.float32)] + [edge] * 4
            + [pltpu.VMEM((2, phases, phases), jnp.float32)] * 2
            + [pltpu.SemaphoreType.DMA((3, levels))] + [pltpu.SemaphoreType.DMA((SWEEPS,))] * 4
            + [pltpu.SemaphoreType.DMA((3,))] * 2,
            compiler_params=pltpu.CompilerParams(
                collective_id=0, has_side_effects=True, vmem_limit_bytes=62 << 20
            ),
            name="sweeps",
        )(inverse_diag, down_block, up_block, reward)

    matrices = P(("grp", "lvl"), None, None)
    columns = P(("grp", "lvl"), "col", None)
    return jax.shard_map(
        local, mesh=mesh, in_specs=(matrices, matrices, matrices, columns),
        out_specs=columns, check_vma=False,
    )
```

```python
import functools

import jax
import jax.numpy as jnp
from jax import lax
from jax.experimental import pallas as pl
from jax.experimental.pallas import tpu as pltpu
from jax.sharding import PartitionSpec as P

SWEEPS = 8
MESH = pl.DeviceIdType.MESH


def split(value):
    high = value.astype(jnp.bfloat16)
    low = (value - high.astype(jnp.float32)).astype(jnp.bfloat16)
    return high, low


def dot(left, right):
    return jnp.dot(left, right, preferred_element_type=jnp.float32)


def apply_split(vector, high, low):
    rows = vector.shape[0]
    rounded = vector.astype(jnp.bfloat16).astype(jnp.float32)
    stacked = jnp.concatenate([rounded, vector - rounded], axis=0).astype(jnp.bfloat16)
    both = dot(stacked, high)
    return both[:rows] + both[rows:] + dot(rounded.astype(jnp.bfloat16), low)


def kernel(
    count, inv_hbm, down_hbm, up_hbm, reward_hbm, out_ref,
    reward_ref, inv, down, up, a_high, a_low, b_high, b_low, base, from_below, from_above, top, bottom,
    edge_out, edge_in,
    reward_sem, load_sem, below_recv, above_recv, top_send, bottom_send, edge_send, edge_recv,
):
    levels = inv_hbm.shape[0]
    place = lax.axis_index("lvl")
    has_below, has_above = place > 0, place < count - 1
    at = dict(device_id_type=MESH)
    end = levels - 1

    def loads(level):
        return [
            pltpu.make_async_copy(source.at[level], target.at[level], load_sem.at[kind, level])
            for kind, (source, target) in enumerate(
                ((inv_hbm, inv), (down_hbm, down), (up_hbm, up))
            )
        ]

    reward_load = pltpu.make_async_copy(reward_hbm, reward_ref, reward_sem)
    for level in range(levels):
        for copy in loads(level):
            copy.start()
        if level == 0:
            reward_load.start()

    barrier = pltpu.get_barrier_semaphore()

    @pl.when(has_below)
    def _():
        pl.semaphore_signal(barrier, inc=1, device_id={"lvl": place - 1}, **at)

    @pl.when(has_above)
    def _():
        pl.semaphore_signal(barrier, inc=1, device_id={"lvl": place + 1}, **at)

    out_ref[...] = jnp.zeros_like(out_ref)
    from_above[0:2] = jnp.zeros_like(from_above[0:2])

    @pl.when(place == 0)
    def _():
        from_below[...] = jnp.zeros_like(from_below)

    @pl.when(place == count - 1)
    def _():
        from_above[...] = jnp.zeros_like(from_above)
        edge_in[...] = jnp.zeros_like(edge_in)
        base[levels] = jnp.zeros_like(base[levels])

    def edge_copies():
        below = {"lvl": place - 1}
        pairs = (
            (base.at[0], base.at[levels]),
            (edge_out.at[0], edge_in.at[0]),
            (edge_out.at[1], edge_in.at[1]),
        )
        return [
            pltpu.make_async_remote_copy(
                src_ref=source, dst_ref=target, send_sem=edge_send.at[n], recv_sem=edge_recv.at[n],
                device_id=below, **at,
            )
            for n, (source, target) in enumerate(pairs)
        ]

    half = levels // 2
    reward_load.wait()
    for level in range(levels):
        if level % half == 0:
            for member in range(level, level + half):
                for copy in loads(member):
                    copy.wait()
        inv_t_high, inv_t_low = split(inv[level].T)
        base[level] = apply_split(reward_ref[level], inv_t_high, inv_t_low)
        for kind, (block, high_ref, low_ref) in enumerate(
            ((down, a_high, a_low), (up, b_high, b_low))
        ):
            block_high, block_low = split(block[level].T)
            product = dot(block_high, inv_t_high) + (
                dot(block_high, inv_t_low) + dot(block_low, inv_t_high)
            )
            high_ref[level], low_ref[level] = split(product)
            if level == 0:
                edge_out[kind] = product
        if level == half - 1:
            pl.semaphore_wait(
                barrier, jnp.minimum(place, 1) + jnp.minimum(count - 1 - place, 1)
            )

            @pl.when(has_below)
            def _():
                for copy in edge_copies():
                    copy.start()

    def going_up(sweep):
        return pltpu.make_async_remote_copy(
            src_ref=top.at[sweep], dst_ref=from_below.at[sweep],
            send_sem=top_send.at[sweep], recv_sem=below_recv.at[sweep],
            device_id={"lvl": place + 1}, **at,
        )

    def going_down(sweep):
        return pltpu.make_async_remote_copy(
            src_ref=bottom.at[sweep], dst_ref=from_above.at[sweep + 2],
            send_sem=bottom_send.at[sweep], recv_sem=above_recv.at[sweep],
            device_id={"lvl": place - 1}, **at,
        )

    def await_below(sweep):
        @pl.when(has_below)
        def _():
            going_up(sweep).wait_recv()

        return from_below[sweep]

    def await_above(turn, sweep):
        @pl.when(has_above & (turn > 0))
        def _():
            going_down(sweep - 2).wait_recv()

        return from_above[sweep]

    def send_up(sweep, value):
        @pl.when(has_above)
        def _():
            top[sweep] = value
            going_up(sweep).start()

    def send_down(turn, sweep, value):
        @pl.when(has_below & (turn < SWEEPS // 2 - 1))
        def _():
            bottom[sweep] = value
            going_down(sweep).start()

    def times_a(value, level):
        return apply_split(value, a_high[level], a_low[level])

    def times_b(value, level):
        return apply_split(value, b_high[level], b_low[level])

    def two_sweeps(turn, _):
        even, odd = 2 * turn, 2 * turn + 1
        terms = [base[n] + times_b(out_ref[n + 1], n) for n in range(end)]
        old_end = out_ref[end]
        x, y = [None] * (levels + 1), [None] * levels

        x[0] = terms[0] + times_a(await_below(even), 0)
        x[1] = terms[1] + times_a(x[0], 1)
        send_down(turn, even, x[1])
        entering = await_below(odd)
        for step in range(2, end):
            low = step - 2
            x[step] = terms[step] + times_a(x[step - 1], step)
            y[low] = (base[low] + times_b(x[low + 1], low)) + times_a(
                entering if low == 0 else y[low - 1], low
            )
            if low == 1:
                send_down(turn, odd, y[1])

        @pl.when(turn == 0)
        def _():
            @pl.when(has_above)
            def _():
                for copy in edge_copies():
                    copy.wait_recv()

            a_high[levels], a_low[levels] = split(edge_in[0])
            b_high[levels], b_low[levels] = split(edge_in[1])

        after = base[levels] + times_a(old_end, levels) + times_b(await_above(turn, even), levels)
        after = jnp.where(turn > 0, after, jnp.zeros_like(after))
        x[end] = (base[end] + times_a(x[end - 1], end)) + times_b(after, end)
        send_up(even, x[end])
        low = end - 2
        y[low] = (base[low] + times_b(x[low + 1], low)) + times_a(y[low - 1], low)
        beyond = base[levels] + times_b(await_above(turn, odd), levels)
        x[levels] = beyond + times_a(x[end], levels)
        low = end - 1
        y[low] = (base[low] + times_b(x[end], low)) + times_a(y[low - 1], low)
        y[end] = (base[end] + times_a(y[end - 1], end)) + times_b(x[levels], end)
        send_up(odd, y[end])
        for n in range(levels):
            out_ref[n] = y[n]
        return 0

    lax.fori_loop(0, SWEEPS // 2, two_sweeps, 0)

    @pl.when(has_above)
    def _():
        for sweep in range(SWEEPS):
            going_up(sweep).wait_send()

    @pl.when(has_below)
    def _():
        for sweep in range(SWEEPS - 2):
            going_down(sweep).wait_send()
        for copy in edge_copies():
            copy.wait_send()


def solution(mesh):
    count = mesh.shape["lvl"]

    def local(inverse_diag, down_block, up_block, reward):
        levels, rows, phases = reward.shape
        whole = (levels, phases, phases)
        wide = pltpu.VMEM(whole, jnp.float32)
        narrow = pltpu.VMEM((levels + 1, phases, phases), jnp.bfloat16)
        edge = pltpu.VMEM((SWEEPS, rows, phases), jnp.float32)
        return pl.pallas_call(
            functools.partial(kernel, count),
            out_shape=jax.ShapeDtypeStruct(reward.shape, jnp.float32),
            in_specs=[pl.BlockSpec(memory_space=pl.ANY)] * 4,
            out_specs=pl.BlockSpec(memory_space=pltpu.VMEM),
            scratch_shapes=[pltpu.VMEM(reward.shape, jnp.float32)] + [wide] * 3 + [narrow] * 4
            + [pltpu.VMEM((levels + 1, rows, phases), jnp.float32)] + [edge] * 4
            + [pltpu.VMEM((2, phases, phases), jnp.float32)] * 2
            + [pltpu.SemaphoreType.DMA, pltpu.SemaphoreType.DMA((3, levels))]
            + [pltpu.SemaphoreType.DMA((SWEEPS,))] * 4
            + [pltpu.SemaphoreType.DMA((3,))] * 2,
            compiler_params=pltpu.CompilerParams(
                collective_id=0, has_side_effects=True, vmem_limit_bytes=62 << 20
            ),
            name="sweeps",
        )(inverse_diag, down_block, up_block, reward)

    matrices = P(("grp", "lvl"), None, None)
    columns = P(("grp", "lvl"), "col", None)
    return jax.shard_map(
        local, mesh=mesh, in_specs=(matrices, matrices, matrices, columns),
        out_specs=columns, check_vma=False,
    )
```

```python
import functools

import jax
import jax.numpy as jnp
from jax import lax
from jax.experimental import pallas as pl
from jax.experimental.pallas import tpu as pltpu
from jax.sharding import PartitionSpec as P

SWEEPS = 8
MESH = pl.DeviceIdType.MESH


def split(value):
    high = value.astype(jnp.bfloat16)
    low = (value - high.astype(jnp.float32)).astype(jnp.bfloat16)
    return high, low


def dot(left, right):
    return jnp.dot(left, right, preferred_element_type=jnp.float32)


def apply_split(vector, high, low):
    rows = vector.shape[0]
    rounded = vector.astype(jnp.bfloat16).astype(jnp.float32)
    stacked = jnp.concatenate([rounded, vector - rounded], axis=0).astype(jnp.bfloat16)
    both = dot(stacked, high)
    return both[:rows] + both[rows:] + dot(rounded.astype(jnp.bfloat16), low)


def kernel(
    count, inv_hbm, down_hbm, up_hbm, reward_hbm, out_ref,
    reward_ref, inv, down, up, a_high, a_low, b_high, b_low, base, from_below, from_above, top, bottom,
    edge_out, edge_in,
    reward_sem, load_sem, below_recv, above_recv, top_send, bottom_send, edge_send, edge_recv,
):
    levels = inv_hbm.shape[0]
    place = lax.axis_index("lvl")
    has_below, has_above = place > 0, place < count - 1
    at = dict(device_id_type=MESH)
    end = levels - 1

    def loads(level):
        return [
            pltpu.make_async_copy(source.at[level], target.at[level], load_sem.at[kind, level])
            for kind, (source, target) in enumerate(
                ((inv_hbm, inv), (down_hbm, down), (up_hbm, up))
            )
        ]

    reward_load = pltpu.make_async_copy(reward_hbm, reward_ref, reward_sem)
    for level in range(levels):
        for copy in loads(level):
            copy.start()
        if level == 0:
            reward_load.start()

    barrier = pltpu.get_barrier_semaphore()

    @pl.when(has_below)
    def _():
        pl.semaphore_signal(barrier, inc=1, device_id={"lvl": place - 1}, **at)

    @pl.when(has_above)
    def _():
        pl.semaphore_signal(barrier, inc=1, device_id={"lvl": place + 1}, **at)

    out_ref[...] = jnp.zeros_like(out_ref)
    from_above[0:2] = jnp.zeros_like(from_above[0:2])

    @pl.when(place == 0)
    def _():
        from_below[...] = jnp.zeros_like(from_below)

    @pl.when(place == count - 1)
    def _():
        from_above[...] = jnp.zeros_like(from_above)
        edge_in[...] = jnp.zeros_like(edge_in)
        base[levels] = jnp.zeros_like(base[levels])

    def edge_copies():
        below = {"lvl": place - 1}
        pairs = (
            (base.at[0], base.at[levels]),
            (edge_out.at[0], edge_in.at[0]),
            (edge_out.at[1], edge_in.at[1]),
        )
        return [
            pltpu.make_async_remote_copy(
                src_ref=source, dst_ref=target, send_sem=edge_send.at[n], recv_sem=edge_recv.at[n],
                device_id=below, **at,
            )
            for n, (source, target) in enumerate(pairs)
        ]

    groups = {0: [0], 1: range(1, levels // 2), levels // 2: range(levels // 2, levels)}
    reward_load.wait()
    for level in range(levels):
        if level in groups:
            for member in groups[level]:
                for copy in loads(member):
                    copy.wait()
        inv_t_high, inv_t_low = split(inv[level].T)
        base[level] = apply_split(reward_ref[level], inv_t_high, inv_t_low)
        for kind, (block, high_ref, low_ref) in enumerate(
            ((down, a_high, a_low), (up, b_high, b_low))
        ):
            block_high, block_low = split(block[level].T)
            product = dot(block_high, inv_t_high) + (
                dot(block_high, inv_t_low) + dot(block_low, inv_t_high)
            )
            high_ref[level], low_ref[level] = split(product)
            if level == 0:
                edge_out[kind] = product
        if level == 0:
            pl.semaphore_wait(
                barrier, jnp.minimum(place, 1) + jnp.minimum(count - 1 - place, 1)
            )

            @pl.when(has_below)
            def _():
                for copy in edge_copies():
                    copy.start()

    def going_up(sweep):
        return pltpu.make_async_remote_copy(
            src_ref=top.at[sweep], dst_ref=from_below.at[sweep],
            send_sem=top_send.at[sweep], recv_sem=below_recv.at[sweep],
            device_id={"lvl": place + 1}, **at,
        )

    def going_down(sweep):
        return pltpu.make_async_remote_copy(
            src_ref=bottom.at[sweep], dst_ref=from_above.at[sweep + 2],
            send_sem=bottom_send.at[sweep], recv_sem=above_recv.at[sweep],
            device_id={"lvl": place - 1}, **at,
        )

    def await_below(sweep):
        @pl.when(has_below)
        def _():
            going_up(sweep).wait_recv()

        return from_below[sweep]

    def await_above(turn, sweep):
        @pl.when(has_above & (turn > 0))
        def _():
            going_down(sweep - 2).wait_recv()

        return from_above[sweep]

    def send_up(sweep, value):
        @pl.when(has_above)
        def _():
            top[sweep] = value
            going_up(sweep).start()

    def send_down(turn, sweep, value):
        @pl.when(has_below & (turn < SWEEPS // 2 - 1))
        def _():
            bottom[sweep] = value
            going_down(sweep).start()

    def times_a(value, level):
        return apply_split(value, a_high[level], a_low[level])

    def times_b(value, level):
        return apply_split(value, b_high[level], b_low[level])

    def two_sweeps(turn, _):
        even, odd = 2 * turn, 2 * turn + 1
        terms = [base[n] + times_b(out_ref[n + 1], n) for n in range(end)]
        old_end = out_ref[end]
        x, y = [None] * (levels + 1), [None] * levels

        x[0] = terms[0] + times_a(await_below(even), 0)
        x[1] = terms[1] + times_a(x[0], 1)
        send_down(turn, even, x[1])
        entering = await_below(odd)
        for step in range(2, end):
            low = step - 2
            x[step] = terms[step] + times_a(x[step - 1], step)
            y[low] = (base[low] + times_b(x[low + 1], low)) + times_a(
                entering if low == 0 else y[low - 1], low
            )
            if low == 1:
                send_down(turn, odd, y[1])

        @pl.when(turn == 0)
        def _():
            @pl.when(has_above)
            def _():
                for copy in edge_copies()[:2]:
                    copy.wait_recv()

            a_high[levels], a_low[levels] = split(edge_in[0])
            b_high[levels] = jnp.zeros_like(b_high[levels])
            b_low[levels] = jnp.zeros_like(b_low[levels])

        @pl.when(turn == 1)
        def _():
            @pl.when(has_above)
            def _():
                edge_copies()[2].wait_recv()

            b_high[levels], b_low[levels] = split(edge_in[1])

        after = base[levels] + times_a(old_end, levels) + times_b(await_above(turn, even), levels)
        after = jnp.where(turn > 0, after, jnp.zeros_like(after))
        x[end] = (base[end] + times_a(x[end - 1], end)) + times_b(after, end)
        send_up(even, x[end])
        low = end - 2
        y[low] = (base[low] + times_b(x[low + 1], low)) + times_a(y[low - 1], low)
        beyond = base[levels] + times_b(await_above(turn, odd), levels)
        x[levels] = beyond + times_a(x[end], levels)
        low = end - 1
        y[low] = (base[low] + times_b(x[end], low)) + times_a(y[low - 1], low)
        y[end] = (base[end] + times_a(y[end - 1], end)) + times_b(x[levels], end)
        send_up(odd, y[end])
        for n in range(levels):
            out_ref[n] = y[n]
        return 0

    lax.fori_loop(0, SWEEPS // 2, two_sweeps, 0)

    @pl.when(has_above)
    def _():
        for sweep in range(SWEEPS):
            going_up(sweep).wait_send()

    @pl.when(has_below)
    def _():
        for sweep in range(SWEEPS - 2):
            going_down(sweep).wait_send()
        for copy in edge_copies():
            copy.wait_send()


def solution(mesh):
    count = mesh.shape["lvl"]

    def local(inverse_diag, down_block, up_block, reward):
        levels, rows, phases = reward.shape
        whole = (levels, phases, phases)
        wide = pltpu.VMEM(whole, jnp.float32)
        narrow = pltpu.VMEM((levels + 1, phases, phases), jnp.bfloat16)
        edge = pltpu.VMEM((SWEEPS, rows, phases), jnp.float32)
        return pl.pallas_call(
            functools.partial(kernel, count),
            out_shape=jax.ShapeDtypeStruct(reward.shape, jnp.float32),
            in_specs=[pl.BlockSpec(memory_space=pl.ANY)] * 4,
            out_specs=pl.BlockSpec(memory_space=pltpu.VMEM),
            scratch_shapes=[pltpu.VMEM(reward.shape, jnp.float32)] + [wide] * 3 + [narrow] * 4
            + [pltpu.VMEM((levels + 1, rows, phases), jnp.float32)] + [edge] * 4
            + [pltpu.VMEM((2, phases, phases), jnp.float32)] * 2
            + [pltpu.SemaphoreType.DMA, pltpu.SemaphoreType.DMA((3, levels))]
            + [pltpu.SemaphoreType.DMA((SWEEPS,))] * 4
            + [pltpu.SemaphoreType.DMA((3,))] * 2,
            compiler_params=pltpu.CompilerParams(
                collective_id=0, has_side_effects=True, vmem_limit_bytes=62 << 20
            ),
            name="sweeps",
        )(inverse_diag, down_block, up_block, reward)

    matrices = P(("grp", "lvl"), None, None)
    columns = P(("grp", "lvl"), "col", None)
    return jax.shard_map(
        local, mesh=mesh, in_specs=(matrices, matrices, matrices, columns),
        out_specs=columns, check_vma=False,
    )
```

```python
import functools

import jax
import jax.numpy as jnp
from jax import lax
from jax.experimental import pallas as pl
from jax.experimental.pallas import tpu as pltpu
from jax.sharding import PartitionSpec as P

SWEEPS = 8
MESH = pl.DeviceIdType.MESH


def split(value):
    high = value.astype(jnp.bfloat16)
    low = (value - high.astype(jnp.float32)).astype(jnp.bfloat16)
    return high, low


def dot(left, right):
    return jnp.dot(left, right, preferred_element_type=jnp.float32)


def apply_split(vector, high, low):
    rows = vector.shape[0]
    rounded = vector.astype(jnp.bfloat16).astype(jnp.float32)
    stacked = jnp.concatenate([rounded, vector - rounded], axis=0).astype(jnp.bfloat16)
    both = dot(stacked, high)
    return both[:rows] + both[rows:] + dot(rounded.astype(jnp.bfloat16), low)


def kernel(
    count, inv_hbm, down_hbm, up_hbm, reward_hbm, out_ref,
    reward_ref, inv, down, up, a_high, a_low, b_high, b_low, base, from_below, from_above, top, bottom,
    edge_out, edge_in,
    reward_sem, load_sem, below_recv, above_recv, top_send, bottom_send, edge_send, edge_recv,
):
    levels = inv_hbm.shape[0]
    place = lax.axis_index("lvl")
    has_below, has_above = place > 0, place < count - 1
    at = dict(device_id_type=MESH)
    end = levels - 1

    def loads(level):
        return [
            pltpu.make_async_copy(source.at[level], target.at[level], load_sem.at[kind, level])
            for kind, (source, target) in enumerate(
                ((inv_hbm, inv), (down_hbm, down), (up_hbm, up))
            )
        ]

    reward_load = pltpu.make_async_copy(reward_hbm, reward_ref, reward_sem)
    for level in range(levels):
        for copy in loads(level):
            copy.start()
        if level == 0:
            reward_load.start()

    barrier = pltpu.get_barrier_semaphore()

    @pl.when(has_below)
    def _():
        pl.semaphore_signal(barrier, inc=1, device_id={"lvl": place - 1}, **at)

    @pl.when(has_above)
    def _():
        pl.semaphore_signal(barrier, inc=1, device_id={"lvl": place + 1}, **at)

    out_ref[...] = jnp.zeros_like(out_ref)
    from_above[0:2] = jnp.zeros_like(from_above[0:2])

    @pl.when(place == 0)
    def _():
        from_below[...] = jnp.zeros_like(from_below)

    @pl.when(place == count - 1)
    def _():
        from_above[...] = jnp.zeros_like(from_above)
        edge_in[...] = jnp.zeros_like(edge_in)
        base[levels] = jnp.zeros_like(base[levels])

    def edge_copies():
        below = {"lvl": place - 1}
        pairs = (
            (base.at[0], base.at[levels]),
            (edge_out.at[0], edge_in.at[0]),
            (edge_out.at[1], edge_in.at[1]),
        )
        return [
            pltpu.make_async_remote_copy(
                src_ref=source, dst_ref=target, send_sem=edge_send.at[n], recv_sem=edge_recv.at[n],
                device_id=below, **at,
            )
            for n, (source, target) in enumerate(pairs)
        ]

    groups = {0: [0], 1: range(1, levels // 2), levels // 2: range(levels // 2, levels)}
    reward_load.wait()
    for level in range(levels):
        if level in groups:
            for member in groups[level]:
                for copy in loads(member):
                    copy.wait()
        inv_t_high, inv_t_low = split(inv[level].T)
        base[level] = apply_split(reward_ref[level], inv_t_high, inv_t_low)
        for kind, (block, high_ref, low_ref) in enumerate(
            ((down, a_high, a_low), (up, b_high, b_low))
        ):
            block_high, block_low = split(block[level].T)
            product = dot(block_high, inv_t_high) + (
                dot(block_high, inv_t_low) + dot(block_low, inv_t_high)
            )
            high_ref[level], low_ref[level] = split(product)
            if level == 0:
                edge_out[kind] = product
                if kind == 0:
                    pl.semaphore_wait(
                        barrier, jnp.minimum(place, 1) + jnp.minimum(count - 1 - place, 1)
                    )

                @pl.when(has_below)
                def _():
                    for copy in edge_copies()[:2] if kind == 0 else edge_copies()[2:]:
                        copy.start()

    def going_up(sweep):
        return pltpu.make_async_remote_copy(
            src_ref=top.at[sweep], dst_ref=from_below.at[sweep],
            send_sem=top_send.at[sweep], recv_sem=below_recv.at[sweep],
            device_id={"lvl": place + 1}, **at,
        )

    def going_down(sweep):
        return pltpu.make_async_remote_copy(
            src_ref=bottom.at[sweep], dst_ref=from_above.at[sweep + 2],
            send_sem=bottom_send.at[sweep], recv_sem=above_recv.at[sweep],
            device_id={"lvl": place - 1}, **at,
        )

    def await_below(sweep):
        @pl.when(has_below)
        def _():
            going_up(sweep).wait_recv()

        return from_below[sweep]

    def await_above(turn, sweep):
        @pl.when(has_above & (turn > 0))
        def _():
            going_down(sweep - 2).wait_recv()

        return from_above[sweep]

    def send_up(sweep, value):
        @pl.when(has_above)
        def _():
            top[sweep] = value
            going_up(sweep).start()

    def send_down(turn, sweep, value):
        @pl.when(has_below & (turn < SWEEPS // 2 - 1))
        def _():
            bottom[sweep] = value
            going_down(sweep).start()

    def times_a(value, level):
        return apply_split(value, a_high[level], a_low[level])

    def times_b(value, level):
        return apply_split(value, b_high[level], b_low[level])

    def two_sweeps(turn, _):
        even, odd = 2 * turn, 2 * turn + 1
        terms = [base[n] + times_b(out_ref[n + 1], n) for n in range(end)]
        old_end = out_ref[end]
        x, y = [None] * (levels + 1), [None] * levels

        x[0] = terms[0] + times_a(await_below(even), 0)
        x[1] = terms[1] + times_a(x[0], 1)
        send_down(turn, even, x[1])
        entering = await_below(odd)
        for step in range(2, end):
            low = step - 2
            x[step] = terms[step] + times_a(x[step - 1], step)
            y[low] = (base[low] + times_b(x[low + 1], low)) + times_a(
                entering if low == 0 else y[low - 1], low
            )
            if low == 1:
                send_down(turn, odd, y[1])

        @pl.when(turn == 0)
        def _():
            @pl.when(has_above)
            def _():
                for copy in edge_copies()[:2]:
                    copy.wait_recv()

            a_high[levels], a_low[levels] = split(edge_in[0])
            b_high[levels] = jnp.zeros_like(b_high[levels])
            b_low[levels] = jnp.zeros_like(b_low[levels])

        @pl.when(turn == 1)
        def _():
            @pl.when(has_above)
            def _():
                edge_copies()[2].wait_recv()

            b_high[levels], b_low[levels] = split(edge_in[1])

        after = base[levels] + times_a(old_end, levels) + times_b(await_above(turn, even), levels)
        after = jnp.where(turn > 0, after, jnp.zeros_like(after))
        x[end] = (base[end] + times_a(x[end - 1], end)) + times_b(after, end)
        send_up(even, x[end])
        low = end - 2
        y[low] = (base[low] + times_b(x[low + 1], low)) + times_a(y[low - 1], low)
        beyond = base[levels] + times_b(await_above(turn, odd), levels)
        x[levels] = beyond + times_a(x[end], levels)
        low = end - 1
        y[low] = (base[low] + times_b(x[end], low)) + times_a(y[low - 1], low)
        y[end] = (base[end] + times_a(y[end - 1], end)) + times_b(x[levels], end)
        send_up(odd, y[end])
        for n in range(levels):
            out_ref[n] = y[n]
        return 0

    lax.fori_loop(0, SWEEPS // 2, two_sweeps, 0)

    @pl.when(has_above)
    def _():
        for sweep in range(SWEEPS):
            going_up(sweep).wait_send()

    @pl.when(has_below)
    def _():
        for sweep in range(SWEEPS - 2):
            going_down(sweep).wait_send()
        for copy in edge_copies():
            copy.wait_send()


def solution(mesh):
    count = mesh.shape["lvl"]

    def local(inverse_diag, down_block, up_block, reward):
        levels, rows, phases = reward.shape
        whole = (levels, phases, phases)
        wide = pltpu.VMEM(whole, jnp.float32)
        narrow = pltpu.VMEM((levels + 1, phases, phases), jnp.bfloat16)
        edge = pltpu.VMEM((SWEEPS, rows, phases), jnp.float32)
        return pl.pallas_call(
            functools.partial(kernel, count),
            out_shape=jax.ShapeDtypeStruct(reward.shape, jnp.float32),
            in_specs=[pl.BlockSpec(memory_space=pl.ANY)] * 4,
            out_specs=pl.BlockSpec(memory_space=pltpu.VMEM),
            scratch_shapes=[pltpu.VMEM(reward.shape, jnp.float32)] + [wide] * 3 + [narrow] * 4
            + [pltpu.VMEM((levels + 1, rows, phases), jnp.float32)] + [edge] * 4
            + [pltpu.VMEM((2, phases, phases), jnp.float32)] * 2
            + [pltpu.SemaphoreType.DMA, pltpu.SemaphoreType.DMA((3, levels))]
            + [pltpu.SemaphoreType.DMA((SWEEPS,))] * 4
            + [pltpu.SemaphoreType.DMA((3,))] * 2,
            compiler_params=pltpu.CompilerParams(
                collective_id=0, has_side_effects=True, vmem_limit_bytes=62 << 20
            ),
            name="sweeps",
        )(inverse_diag, down_block, up_block, reward)

    matrices = P(("grp", "lvl"), None, None)
    columns = P(("grp", "lvl"), "col", None)
    return jax.shard_map(
        local, mesh=mesh, in_specs=(matrices, matrices, matrices, columns),
        out_specs=columns, check_vma=False,
    )
```
